32 devices in a mesh: groups: 2 (over y), src: 8 (over z, x), tgt: 2 (over core).
Axes of the slice: x: 2, y: 2, z: 4, core: 2. Of those that a mesh axis runs over, the one named last changes fastest.
Arguments:
- source_points: bfloat16 [256, 64, 128], P(('groups', 'src')), parts along dimension 0, may hold values from -1.1 to 1.1
- target_points: bfloat16 [192, 64, 128], P(('groups', 'tgt')), parts along dimension 0, may hold values from -1.1 to 1.1
- source_logmass: float32 [32768], P(('groups', 'src')), parts along dimension 0, may hold values from -3 to 3
- target_logmass: float32 [24576], P(('groups', 'tgt')), parts along dimension 0, may hold values from -3 to 3
- warm_potential: float32 [24576], P(('groups', 'tgt')), parts along dimension 0, may hold values from -4 to 4
- block_ids: int32 [256, 2, 16], P(('groups', 'src'), 'tgt'), parts along dimension 0, may hold values from 0 to 47, as said below
- live_counts: int32 [256, 2], P(('groups', 'src'), 'tgt'), parts along dimension 0, may hold values from 1 to 16, as said below
Outputs:
- source_potential: float32 [32768], P(('groups', 'src')), parts along dimension 0
- target_potential: float32 [24576], P(('groups', 'tgt')), parts along dimension 0
The draws below stay inside these ranges and needn't reach their ends.
There are 2 independent parts, one for each index of `groups`. The reference program is written for one: setup_inputs(seed, part) draws one part's arguments, and reference() takes and returns one part's arrays. A program takes and returns all parts, laid end to end along the dimension named above; each array names one. Nothing has to cross between parts.
Inputs may be any that keep to these rules, and one draw needn't show every extreme that they name: `block_ids`: the 16 ids of one source block and one target half are distinct; only the first live_counts slots belong to the support. A half may hold target blocks that no live slot names. `live_counts`: some source block has all 16 slots of its first half live.
All inputs are finite; a program needn't handle non-finite values.
Results may differ from the reference program's by a relative error of at most 0.0003.
Values sent between devices are 32-bit elements; how exact they have to be, the bound alone decides.
No kernel may reach another device: no remote copies, remote signals or barrier semaphores. Data moves between devices by JAX's collectives and lax.ppermute only.
A program may use at most 64 MiB of HBM per device.

```python
import jax
import jax.numpy as jnp
from jax import lax

F = 64
BLK = 128
KH = 16
ITERS = 2
RB_DEV = 16
TB_HALF = 48
HALVES = 2
NRB = 128
NS = 16384
NTB = 96
NT = 12288


def point_cloud(key, block_total):
    spread = 0.18
    values = jnp.clip(jax.random.normal(key, (block_total, F, BLK), jnp.float32), -6.0, 6.0)
    return (spread * values).astype(jnp.bfloat16)


def draw_source_points(key, part):
    return point_cloud(jax.random.fold_in(key, 1), NRB)


def draw_target_points(key, part):
    return point_cloud(jax.random.fold_in(key, 2), NTB)


def draw_live_counts(key, part):
    density = jax.random.randint(jax.random.fold_in(key, 21), (NRB // RB_DEV, 1), 0, KH)
    density = jnp.repeat(density, RB_DEV, axis=0)
    second_factor = jax.random.randint(jax.random.fold_in(key, 22), (NRB, HALVES), 0, KH)
    counts = jnp.minimum(KH, 1 + density * second_factor // max(KH // 2, 1))
    chosen_row = jax.random.randint(jax.random.fold_in(key, 23), (), 0, NRB)
    return counts.at[chosen_row, 0].set(KH).astype(jnp.int32)


def draw_block_ids(key, part):
    random_keys = jax.random.randint(jax.random.fold_in(key, 31), (NRB, HALVES, TB_HALF), 0, 1 << 20)
    excluded = jax.random.randint(jax.random.fold_in(key, 32), (HALVES,), 0, TB_HALF)
    positions = jnp.arange(TB_HALF, dtype=jnp.int32)
    scores = random_keys * TB_HALF + positions
    barred = positions[None, None, :] == excluded[None, :, None]
    scores = jnp.where(barred, 1 << 30, scores)
    return jnp.argsort(scores, axis=-1)[:, :, :KH].astype(jnp.int32)


def shard_levels(stream_key, dims, cuts, smallest, high):
    def one(axis_at, blocks):
        steps = jax.random.uniform(jax.random.fold_in(jax.random.fold_in(stream_key, 6), axis_at), (blocks,), jnp.float32, smallest / len(cuts), high / len(cuts))
        return jnp.repeat(jnp.exp(steps), dims[axis_at] // blocks).reshape((-1,) + (1,) * (len(dims) - axis_at - 1))

    loudness = one(*cuts[0])
    for cut in cuts[1:]:
        loudness = loudness * one(*cut)
    return loudness


def centred(stream_key, shape, deviation, bound, cuts=(), kind=jnp.bfloat16):
    drawn = jax.random.normal(stream_key, shape, jnp.float32) * deviation
    if len(cuts) > 0:
        drawn = shard_levels(stream_key, shape, cuts, -0.22, 0.18) * drawn
    return jnp.clip(drawn, min=-bound, max=bound).astype(kind)


def setup_inputs(seed: int = 0, part: int = 0) -> dict:
    splits = jax.random.split(jax.random.key(seed), 8)
    part_keys = jax.random.split(jax.random.fold_in(splits[7], part), 8)
    return {
        "source_points": draw_source_points(jax.random.fold_in(jax.random.fold_in(splits[7], part), 71), part),
        "target_points": draw_target_points(jax.random.fold_in(jax.random.fold_in(splits[7], part), 71), part),
        "source_logmass": jnp.clip(jax.random.uniform(part_keys[2], (NS,), jnp.float32, -3.0, 3.0) * shard_levels(part_keys[2], (NS,), ((0, 8),), -0.4, 0.0), -3.0, 3.0),
        "target_logmass": jnp.clip(jax.random.uniform(part_keys[3], (NT,), jnp.float32, -3.0, 3.0) * shard_levels(part_keys[3], (NT,), ((0, 2),), -0.4, 0.0), -3.0, 3.0),
        "warm_potential": centred(part_keys[4], (NT,), 1.0, 4.0, ((0, 2),), jnp.float32),
        "block_ids": draw_block_ids(jax.random.fold_in(jax.random.fold_in(splits[7], part), 71), part),
        "live_counts": draw_live_counts(jax.random.fold_in(jax.random.fold_in(splits[7], part), 71), part),
    }


epsilon = 0.1
lowest = -1.0e30
reach_limit = -1.0e29


def reference(source_points, target_points, source_logmass, target_logmass, warm_potential, block_ids, live_counts):
    sources = source_points.astype(jnp.float32)
    targets = target_points.astype(jnp.float32)
    source_sq = jnp.sum(sources * sources, axis=1)
    target_sq = jnp.sum(targets * targets, axis=1)
    half_base = (jnp.arange(HALVES, dtype=jnp.int32) * TB_HALF)[None, :, None]
    global_ids = (block_ids + half_base).reshape(NRB, HALVES * KH)
    live_slots = (jnp.arange(KH, dtype=jnp.int32)[None, None, :] < live_counts[:, :, None]).reshape(NRB, HALVES * KH)
    source_mass = source_logmass.reshape(NRB, BLK)
    target_mass = target_logmass.reshape(NTB, BLK)
    potential = warm_potential.reshape(NTB, BLK)
    row_index = jnp.arange(NRB, dtype=jnp.int32)
    segment_ids = jnp.where(live_slots, global_ids, NTB).reshape(-1).astype(jnp.int32)

    def block_costs(row_block):
        chosen = global_ids[row_block]
        products = jnp.einsum("dr,kdc->krc", sources[row_block], targets[chosen], precision=lax.Precision.HIGHEST)
        return source_sq[row_block][None, :, None] + target_sq[chosen][:, None, :] - 2.0 * products

    source_potential = jnp.zeros((NRB, BLK), jnp.float32)
    for sweep_index in range(ITERS):
        def row_update(row_block):
            scores = (potential[global_ids[row_block]][:, None, :] - block_costs(row_block)) / epsilon
            keep = live_slots[row_block][:, None, None]
            scores = jnp.where(keep, scores, lowest)
            best = jnp.max(scores, axis=(0, 2))
            total = jnp.sum(jnp.where(keep, jnp.exp(scores - best[None, :, None]), 0.0), axis=(0, 2))
            return epsilon * source_mass[row_block] - epsilon * (best + jnp.log(total))

        source_potential = lax.map(row_update, row_index)

        def column_tiles(row_block):
            scores = (source_potential[row_block][None, :, None] - block_costs(row_block)) / epsilon
            tile_max = jnp.max(scores, axis=1)
            tile_sum = jnp.sum(jnp.exp(scores - tile_max[:, None, :]), axis=1)
            keep = live_slots[row_block][:, None]
            return jnp.where(keep, tile_max, lowest), jnp.where(keep, tile_sum, 0.0)

        tile_max, tile_sum = lax.map(column_tiles, row_index)
        tile_max = tile_max.reshape(-1, BLK)
        tile_sum = tile_sum.reshape(-1, BLK)
        best = jax.ops.segment_max(tile_max, segment_ids, num_segments=NTB + 1)
        total = jax.ops.segment_sum(tile_sum * jnp.exp(tile_max - best[segment_ids]), segment_ids, num_segments=NTB + 1)
        best = best[:NTB]
        total = total[:NTB]
        reached = best > reach_limit
        log_total = jnp.where(reached, best + jnp.log(jnp.where(reached, total, 1.0)), 0.0)
        potential = epsilon * target_mass - epsilon * log_total
    return source_potential.reshape(-1), potential.reshape(-1)
```

```python
import functools
import math

import jax
import jax.numpy as jnp
from jax import lax
from jax.experimental import pallas as pl
from jax.experimental.pallas import tpu as pltpu
from jax.sharding import PartitionSpec as P

ITERS = 2
epsilon = 0.1
lowest = -1.0e30
reach_limit = -1.0e29

LOG2E = math.log2(math.e)
SCALE = LOG2E / epsilon
UNSCALE = epsilon / LOG2E
SHIFT = 60.0
SUM_LOW = 2.0**-30
SUM_HIGH = 2.0**126
WEIGHT_LOW = 2.0**-125
GROUP = 4


def log_add(first, second):
    highest = jnp.maximum(first, second)
    return highest + jnp.log2(jnp.exp2(first - highest) + jnp.exp2(second - highest))


def log_sum(parts):
    highest = functools.reduce(jnp.maximum, parts)
    total = functools.reduce(jnp.add, [jnp.exp2(part - highest) for part in parts])
    return highest + jnp.log2(total)


def out_of_range(sums, mask=None):
    good = (sums >= SUM_LOW) & (sums <= SUM_HIGH)
    if mask is not None:
        good = good | jnp.logical_not(mask)
    return jnp.max(jnp.where(good, 0.0, 1.0)) > 0.5


def make_kernels(rows, targets, slots, feat, blk):
    per_row = slots // GROUP
    groups = rows * per_row
    padded = targets + 8

    def slot(ids, counts, code, u):
        row = code // per_row
        row_at = jnp.minimum(row, rows - 1)
        k = (code % per_row) * GROUP + u
        target = ids[row_at, k]
        live = (row < rows) & (k < counts[row_at, 0])
        return row, row_at, target, jnp.where(live, target, targets)

    def tile_scores(x, y, row, target):
        return lax.dot_general(
            x[row], y[target], (((0,), (0,)), ((), ())), preferred_element_type=jnp.float32
        ) * (2.0 * SCALE)

    def slow_rows(ids, counts, x_hbm, y_hbm, weight_log, out):
        def run(x, y):
            pltpu.sync_copy(x_hbm, x)
            pltpu.sync_copy(y_hbm, y)

            @pl.loop(0, rows)
            def _(row):
                def body(k, state):
                    target = ids[row, k]
                    score = tile_scores(x, y, row, target) + weight_log[pl.ds(target, 1), :]
                    score = score.T
                    best = jnp.maximum(state[0], jnp.max(score, axis=0, keepdims=True))
                    total = state[1] * jnp.exp2(state[0] - best)
                    total += jnp.sum(jnp.exp2(score - best), axis=0, keepdims=True)
                    return best, total

                start = (jnp.full((1, blk), lowest, jnp.float32), jnp.zeros((1, blk), jnp.float32))
                best, total = lax.fori_loop(0, counts[row, 0], body, start)
                out[pl.ds(row, 1), :] = best + jnp.log2(total)

        pl.run_scoped(
            run,
            pltpu.VMEM((rows, feat, blk), jnp.bfloat16),
            pltpu.VMEM((targets, feat, blk), jnp.bfloat16),
        )

    def slow_columns(ids, counts, x_hbm, y_hbm, weight_log, out):
        def run(x, y, total):
            pltpu.sync_copy(x_hbm, x)
            pltpu.sync_copy(y_hbm, y)
            out[...] = jnp.full((targets, blk), lowest, jnp.float32)
            total[...] = jnp.zeros((targets, blk), jnp.float32)

            @pl.loop(0, rows)
            def _(row):
                @pl.loop(0, counts[row, 0])
                def _(k):
                    target = ids[row, k]
                    score = (tile_scores(x, y, row, target).T + weight_log[pl.ds(row, 1), :]).T
                    old = out[pl.ds(target, 1), :]
                    best = jnp.maximum(old, jnp.max(score, axis=0, keepdims=True))
                    add = jnp.sum(jnp.exp2(score - best), axis=0, keepdims=True)
                    total[pl.ds(target, 1), :] = (
                        total[pl.ds(target, 1), :] * jnp.exp2(old - best) + add
                    )
                    out[pl.ds(target, 1), :] = best

            best = out[...]
            reached = best > reach_limit
            out[...] = jnp.where(
                reached, best + jnp.log2(jnp.where(reached, total[...], 1.0)), lowest
            )

        pl.run_scoped(
            run,
            pltpu.VMEM((rows, feat, blk), jnp.bfloat16),
            pltpu.VMEM((targets, feat, blk), jnp.bfloat16),
            pltpu.VMEM((targets, blk), jnp.float32),
        )

    def list_groups(counts, work):
        def add(row, n):
            for g in range(per_row):
                work[n + g] = row * per_row + g
            return n + (counts[row, 0] + GROUP - 1) // GROUP

        n = lax.fori_loop(0, rows, add, 0)
        for g in range(4):
            work[n + g] = groups
        return n

    def row_weights(log_weight, weights):
        top = jnp.max(log_weight)
        values = jnp.exp2(log_weight - (top - SHIFT))
        weights[0:targets, :] = values
        weights[targets:padded, :] = jnp.zeros((padded - targets, blk), jnp.float32)
        return top, jnp.min(values) < WEIGHT_LOW

    def finish_rows(acc, top, flushed, log_weight, ids, counts, x_hbm, y_hbm, out, sums):
        for row in range(rows):
            sums[row : row + 1, :] = jnp.sum(acc[row].T, axis=0, keepdims=True)
        found = sums[...]
        out[...] = jnp.log2(found) + (top - SHIFT)

        @pl.when(flushed | out_of_range(found))
        def _():
            slow_rows(ids, counts, x_hbm, y_hbm, log_weight, out)

    def first_rows(
        ids, counts, x, y, x_hbm, y_hbm, warm,
        out, tiles, target_sq, member, work, n_work,
        acc, weights, log_weight, x_rows, even, odd, sums,
    ):
        n = list_groups(counts, work)
        n_work[0] = n
        for target in range(targets):
            values = y[target].astype(jnp.float32)
            target_sq[target : target + 1, :] = jnp.sum(values * values, axis=0, keepdims=True)
        log_weight[...] = (warm[...] - target_sq[...]) * SCALE
        top, flushed = row_weights(log_weight[...], weights)
        member[...] = jnp.zeros(member.shape, jnp.float32)
        for row in range(rows):
            x_rows[row] = x[row].T
        acc[...] = jnp.zeros(acc.shape, jnp.float32)

        def products(code, buffer):
            for u in range(GROUP):
                _, row_at, target, _ = slot(ids, counts, code, u)
                buffer[u] = jnp.dot(x_rows[row_at], y[target], preferred_element_type=jnp.float32)

        def consume(code, buffer):
            row = code // per_row
            total = acc[row]
            for u in range(GROUP):
                _, _, _, weight_at = slot(ids, counts, code, u)
                value = jnp.exp2(buffer[u] * (2.0 * SCALE))
                tiles[code * GROUP + u] = value
                total += value * weights[pl.ds(weight_at, 1), :]
                member[pl.ds(weight_at, 1), :] = jnp.ones((1, blk), jnp.float32)
            acc[row] = total

        products(work[0], even)

        @pl.loop(0, (n + 1) // 2)
        def _(pair):
            products(work[2 * pair + 1], odd)
            consume(work[2 * pair], even)
            products(work[2 * pair + 2], even)
            consume(work[2 * pair + 1], odd)

        finish_rows(acc, top, flushed, log_weight, ids, counts, x_hbm, y_hbm, out, sums)

    def later_rows(
        ids, counts, work, n_work, tiles, x_hbm, y_hbm, parts, target_mass, target_sq,
        out,
        acc, weights, log_weight, sums,
    ):
        merged = parts[...]
        reached = merged > reach_limit
        log_weight[...] = target_mass[...] * LOG2E - jnp.where(
            reached, merged, target_sq[...] * SCALE
        )
        top, flushed = row_weights(log_weight[...], weights)
        acc[...] = jnp.zeros(acc.shape, jnp.float32)

        def consume(code):
            row = code // per_row
            total = acc[row]
            for u in range(GROUP):
                _, _, _, weight_at = slot(ids, counts, code, u)
                total += tiles[code * GROUP + u] * weights[pl.ds(weight_at, 1), :]
            acc[row] = total

        @pl.loop(0, (n_work[0] + 1) // 2)
        def _(pair):
            consume(work[2 * pair])
            consume(work[2 * pair + 1])

        finish_rows(acc, top, flushed, log_weight, ids, counts, x_hbm, y_hbm, out, sums)

    def columns(
        last, ids, counts, work, n_work, tiles, x_hbm, y_hbm, own, other, source_mass, member,
        *rest,
    ):
        if last:
            x, out, potential, acc, weights, sums, log_weight = rest
        else:
            out, acc, weights, sums, log_weight = rest
        log_weight[...] = source_mass[...] * LOG2E - log_add(own[...], other[...])
        if last:
            for row in range(rows):
                values = x[row].astype(jnp.float32)
                source_sq = jnp.sum(values * values, axis=0, keepdims=True)
                potential[row : row + 1, :] = log_weight[row : row + 1, :] * UNSCALE + source_sq
        top = jnp.max(log_weight[...])
        values = jnp.exp2(log_weight[...] - (top - SHIFT))
        flushed = jnp.min(values) < WEIGHT_LOW
        for row in range(rows):
            weights[row] = jnp.broadcast_to(values[row : row + 1, :], (blk, blk)).T
        acc[...] = jnp.zeros(acc.shape, jnp.float32)

        def consume(code):
            row_at = jnp.minimum(code // per_row, rows - 1)
            weight = weights[row_at]
            for u in range(GROUP):
                _, _, _, target = slot(ids, counts, code, u)
                value = (tiles[code * GROUP + u] * weight).reshape(blk // 8, 8, blk)
                acc[target] += jnp.sum(value, axis=0)

        @pl.loop(0, (n_work[0] + 1) // 2)
        def _(pair):
            consume(work[2 * pair])
            consume(work[2 * pair + 1])

        for target in range(targets):
            sums[target : target + 1, :] = jnp.sum(acc[target], axis=0, keepdims=True)
        found = sums[...]
        reached = member[0:targets, :] > 0.5
        out[...] = jnp.where(
            reached, jnp.log2(jnp.where(reached, found, 1.0)) + (top - SHIFT), lowest
        )

        @pl.when(flushed | out_of_range(found, reached))
        def _():
            slow_columns(ids, counts, x_hbm, y_hbm, log_weight, out)

    smem = pl.BlockSpec(memory_space=pltpu.SMEM)
    vmem = pl.BlockSpec(memory_space=pltpu.VMEM)
    anywhere = pl.BlockSpec(memory_space=pl.ANY)
    f32 = jnp.float32
    limit = pltpu.CompilerParams(vmem_limit_bytes=20 * 1024 * 1024)

    first_rows_call = pl.pallas_call(
        first_rows,
        name="first_rows",
        in_specs=[smem, smem, vmem, vmem, anywhere, anywhere, vmem],
        out_specs=[vmem, vmem, vmem, vmem, smem, smem],
        out_shape=[
            jax.ShapeDtypeStruct((rows, blk), f32),
            pltpu.VMEM(((groups + 1) * GROUP, blk, blk), f32),
            jax.ShapeDtypeStruct((targets, blk), f32),
            jax.ShapeDtypeStruct((padded, blk), f32),
            jax.ShapeDtypeStruct((groups + 8,), jnp.int32),
            jax.ShapeDtypeStruct((1,), jnp.int32),
        ],
        scratch_shapes=[
            pltpu.VMEM((rows + 1, blk, blk), f32),
            pltpu.VMEM((padded, blk), f32),
            pltpu.VMEM((targets, blk), f32),
            pltpu.VMEM((rows, blk, feat), jnp.bfloat16),
            pltpu.VMEM((GROUP, blk, blk), f32),
            pltpu.VMEM((GROUP, blk, blk), f32),
            pltpu.VMEM((rows, blk), f32),
        ],
        compiler_params=limit,
    )
    later_rows_call = pl.pallas_call(
        later_rows,
        name="later_rows",
        in_specs=[smem, smem, smem, smem, vmem, anywhere, anywhere, vmem, vmem, vmem],
        out_specs=vmem,
        out_shape=jax.ShapeDtypeStruct((rows, blk), f32),
        scratch_shapes=[
            pltpu.VMEM((rows + 1, blk, blk), f32),
            pltpu.VMEM((padded, blk), f32),
            pltpu.VMEM((targets, blk), f32),
            pltpu.VMEM((rows, blk), f32),
        ],
        compiler_params=limit,
    )

    def columns_call(last):
        outs = [jax.ShapeDtypeStruct((targets, blk), f32)]
        if last:
            outs.append(jax.ShapeDtypeStruct((rows, blk), f32))
        return pl.pallas_call(
            functools.partial(columns, last),
            name="last_columns" if last else "columns",
            in_specs=[smem] * 4 + [vmem, anywhere, anywhere] + [vmem] * (5 if last else 4),
            out_specs=[vmem] * len(outs),
            out_shape=outs,
            scratch_shapes=[
                pltpu.VMEM((padded, 8, blk), f32),
                pltpu.VMEM((rows, blk, blk), f32),
                pltpu.VMEM((targets, blk), f32),
                pltpu.VMEM((rows, blk), f32),
            ],
            compiler_params=limit,
        )

    return first_rows_call, later_rows_call, columns_call


def joined_over_sources(part):
    size = lax.axis_size("src")
    step = 1
    while step < size:
        width = 4 if step == 1 and size % 4 == 0 else 2
        parts = [part] + [
            lax.ppermute(part, "src", [(i, i ^ (step * k)) for i in range(size)])
            for k in range(1, width)
        ]
        part = log_sum(parts)
        step *= width
    return part


def per_device(
    source_points,
    target_points,
    source_logmass,
    target_logmass,
    warm_potential,
    block_ids,
    live_counts,
):
    rows, feat, blk = source_points.shape
    targets = target_points.shape[0]
    slots = block_ids.shape[2]
    ids = block_ids.reshape(rows, slots)
    source_mass = source_logmass.reshape(rows, blk)
    target_mass = target_logmass.reshape(targets, blk)
    warm = warm_potential.reshape(targets, blk)
    first_rows, later_rows, columns = make_kernels(rows, targets, slots, feat, blk)
    swap = [(i, i ^ 1) for i in range(lax.axis_size("tgt"))]

    part, tiles, target_sq, member, work, n_work = first_rows(
        ids, live_counts, source_points, target_points, source_points, target_points, warm
    )
    tiles = pltpu.with_memory_space_constraint(tiles, pltpu.VMEM)
    for sweep_index in range(ITERS):
        last = sweep_index == ITERS - 1
        common = (ids, live_counts, work, n_work, tiles, source_points, target_points)
        if sweep_index > 0:
            part = later_rows(*common, merged, target_mass, target_sq)
        other = lax.ppermute(part, "tgt", swap)
        found = columns(last)(
            *common, part, other, source_mass, member, *([source_points] if last else [])
        )
        merged = joined_over_sources(found[0])
    source_potential = found[1]
    log_total = jnp.where(
        merged > reach_limit, merged * UNSCALE - target_sq, 0.0
    )
    potential = epsilon * target_mass - log_total
    return (source_potential.reshape(-1), potential.reshape(-1))


def solution(mesh):
    in_specs = (
        P(("groups", "src"), None, None),
        P(("groups", "tgt"), None, None),
        P(("groups", "src")),
        P(("groups", "tgt")),
        P(("groups", "tgt")),
        P(("groups", "src"), "tgt", None),
        P(("groups", "src"), "tgt"),
    )
    out_specs = (P(("groups", "src")), P(("groups", "tgt")))
    return jax.shard_map(
        per_device, mesh=mesh, in_specs=in_specs, out_specs=out_specs, check_vma=False
    )
```

```python
import functools
import math

import jax
import jax.numpy as jnp
from jax import lax
from jax.experimental import pallas as pl
from jax.experimental.pallas import tpu as pltpu
from jax.sharding import PartitionSpec as P

ITERS = 2
epsilon = 0.1
lowest = -1.0e30
reach_limit = -1.0e29

LOG2E = math.log2(math.e)
SCALE = LOG2E / epsilon
UNSCALE = epsilon / LOG2E
SHIFT = 60.0
SUM_LOW = 2.0**-30
SUM_HIGH = 2.0**126
WEIGHT_LOW = 2.0**-125
GROUP = 4
STEP = 4
ROWS_STEP = 2


def log_add(first, second):
    highest = jnp.maximum(first, second)
    return highest + jnp.log2(jnp.exp2(first - highest) + jnp.exp2(second - highest))


def log_sum(parts):
    highest = functools.reduce(jnp.maximum, parts)
    total = functools.reduce(jnp.add, [jnp.exp2(part - highest) for part in parts])
    return highest + jnp.log2(total)


def make_kernels(rows, targets, slots, feat, blk):
    per_row = slots // GROUP
    groups = rows * per_row
    padded = targets + 8

    def tile_scores(x, y, row, target):
        return lax.dot_general(
            x[row], y[target], (((0,), (0,)), ((), ())), preferred_element_type=jnp.float32
        ) * (2.0 * SCALE)

    def slow_rows(ids, counts, x_hbm, y_hbm, weight_log, out):
        def run(x, y):
            pltpu.sync_copy(x_hbm, x)
            pltpu.sync_copy(y_hbm, y)

            @pl.loop(0, rows)
            def _(row):
                def body(k, state):
                    target = ids[row, k]
                    score = tile_scores(x, y, row, target) + weight_log[pl.ds(target, 1), :]
                    score = score.T
                    best = jnp.maximum(state[0], jnp.max(score, axis=0, keepdims=True))
                    total = state[1] * jnp.exp2(state[0] - best)
                    total += jnp.sum(jnp.exp2(score - best), axis=0, keepdims=True)
                    return best, total

                start = (jnp.full((1, blk), lowest, jnp.float32), jnp.zeros((1, blk), jnp.float32))
                best, total = lax.fori_loop(0, counts[row], body, start)
                out[pl.ds(row, 1), :] = best + jnp.log2(total)

        pl.run_scoped(
            run,
            pltpu.VMEM((rows, feat, blk), jnp.bfloat16),
            pltpu.VMEM((targets, feat, blk), jnp.bfloat16),
        )

    def slow_columns(ids, counts, x_hbm, y_hbm, weight_log, out):
        def run(x, y, total):
            pltpu.sync_copy(x_hbm, x)
            pltpu.sync_copy(y_hbm, y)
            out[...] = jnp.full((targets, blk), lowest, jnp.float32)
            total[...] = jnp.zeros((targets, blk), jnp.float32)

            @pl.loop(0, rows)
            def _(row):
                @pl.loop(0, counts[row])
                def _(k):
                    target = ids[row, k]
                    score = (tile_scores(x, y, row, target).T + weight_log[pl.ds(row, 1), :]).T
                    old = out[pl.ds(target, 1), :]
                    best = jnp.maximum(old, jnp.max(score, axis=0, keepdims=True))
                    add = jnp.sum(jnp.exp2(score - best), axis=0, keepdims=True)
                    total[pl.ds(target, 1), :] = (
                        total[pl.ds(target, 1), :] * jnp.exp2(old - best) + add
                    )
                    out[pl.ds(target, 1), :] = best

            best = out[...]
            reached = best > reach_limit
            out[...] = jnp.where(
                reached, best + jnp.log2(jnp.where(reached, total[...], 1.0)), lowest
            )

        pl.run_scoped(
            run,
            pltpu.VMEM((rows, feat, blk), jnp.bfloat16),
            pltpu.VMEM((targets, feat, blk), jnp.bfloat16),
            pltpu.VMEM((targets, blk), jnp.float32),
        )

    def list_groups(counts, work):
        def add(row, n):
            for g in range(per_row):
                work[n + g] = row * per_row + g
            return n + (counts[row] + GROUP - 1) // GROUP

        n = lax.fori_loop(0, rows, add, 0)
        for g in range(STEP):
            work[n + g] = groups
        work[groups + STEP] = (n + STEP - 1) // STEP

    def largest(values):
        return jnp.max(values, keepdims=True)

    def row_weights(log_weight, weights):
        top = largest(log_weight)
        values = jnp.exp2(log_weight - (top - SHIFT))
        weights[0:targets, :] = values
        weights[targets:padded, :] = jnp.zeros((padded - targets, blk), jnp.float32)
        return top, jnp.min(values, keepdims=True)

    def bad(sums, least, mask=None):
        good = (sums >= SUM_LOW) & (sums <= SUM_HIGH)
        if mask is not None:
            good = good | jnp.logical_not(mask)
        good = good & (least >= WEIGHT_LOW)
        return jnp.max(jnp.where(good, 0.0, 1.0)) > 0.5

    def finish_rows(acc, top, least, log_weight, ids, counts, x_hbm, y_hbm, out, sums):
        for row in range(rows):
            sums[row : row + 1, :] = jnp.sum(acc[row].T, axis=0, keepdims=True)
        found = sums[...]
        out[...] = jnp.log2(found) + (top - SHIFT)

        @pl.when(bad(found, least))
        def _():
            slow_rows(ids, counts, x_hbm, y_hbm, log_weight, out)

    def first_rows(
        ids_hbm, counts_hbm, x_hbm, y_hbm, warm_hbm, source_mass_hbm, target_mass_hbm,
        out, tiles, target_sq, source_sq, member, source_mass, target_mass, ids, counts, work, where_to,
        x, y, warm, acc, weights, log_weight, x_rows, sums, sems,
    ):
        copies = [
            pltpu.make_async_copy(source, target, sems.at[i])
            for i, (source, target) in enumerate(
                (
                    (y_hbm, y),
                    (x_hbm, x),
                    (warm_hbm, warm),
                    (ids_hbm, ids),
                    (counts_hbm, counts),
                    (source_mass_hbm, source_mass),
                    (target_mass_hbm, target_mass),
                )
            )
        ]
        for copy in copies:
            copy.start()
        member[...] = jnp.zeros(member.shape, jnp.float32)
        for copy in copies:
            copy.wait()
        list_groups(counts, work)
        for u in range(GROUP):
            where_to[groups * GROUP + u] = targets
        for target in range(targets):
            values = y[target].astype(jnp.float32)
            target_sq[target : target + 1, :] = jnp.sum(values * values, axis=0, keepdims=True)
        log_weight[...] = (warm[...] - target_sq[...]) * SCALE
        top, least = row_weights(log_weight[...], weights)
        for row in range(rows):
            values = x[row].astype(jnp.float32)
            source_sq[row : row + 1, :] = jnp.sum(values * values, axis=0, keepdims=True)
            x_rows[row] = x[row].T

        @pl.loop(0, rows // ROWS_STEP)
        def _(step):
            for part in range(ROWS_STEP):
                row = step * ROWS_STEP + part
                count = counts[row]
                total = jnp.zeros((blk, blk), jnp.float32)
                for k in range(slots):
                    target = ids[row, k]
                    place = jnp.where(k < count, target, targets)
                    where_to[row * slots + k] = place
                    product = jnp.dot(x_rows[row], y[target], preferred_element_type=jnp.float32)
                    value = jnp.exp2(product * (2.0 * SCALE))
                    tiles[row * slots + k] = value
                    total += value * weights[pl.ds(place, 1), :]
                    member[pl.ds(place, 1), :] = jnp.ones((1, blk), jnp.float32)
                acc[row] = total

        finish_rows(acc, top, least, log_weight, ids, counts, x_hbm, y_hbm, out, sums)

    def later_rows(
        ids, counts, work, where_to, tiles, x_hbm, y_hbm, merged_ref, target_mass, target_sq,
        out,
        acc, weights, log_weight, sums,
    ):
        merged = merged_ref[...]
        reached = merged > reach_limit
        log_weight[...] = target_mass[...] * LOG2E - jnp.where(
            reached, merged, target_sq[...] * SCALE
        )
        top, least = row_weights(log_weight[...], weights)
        acc[...] = jnp.zeros(acc.shape, jnp.float32)

        @pl.loop(0, work[groups + STEP])
        def _(step):
            for g in range(STEP):
                code = work[step * STEP + g]
                row = code // per_row
                total = acc[row]
                for u in range(GROUP):
                    place = where_to[code * GROUP + u]
                    total += tiles[code * GROUP + u] * weights[pl.ds(place, 1), :]
                acc[row] = total

        finish_rows(acc, top, least, log_weight, ids, counts, x_hbm, y_hbm, out, sums)

    def columns(
        last, ids, counts, work, where_to, tiles, x_hbm, y_hbm, own, other, source_mass, member,
        *rest,
    ):
        if last:
            source_sq, out, potential, acc, weights, sums, log_weight = rest
        else:
            out, acc, weights, sums, log_weight = rest
        log_weight[...] = source_mass[...] * LOG2E - log_add(own[...], other[...])
        if last:
            potential[...] = log_weight[...] * UNSCALE + source_sq[...]
        top = largest(log_weight[...])
        values = jnp.exp2(log_weight[...] - (top - SHIFT))
        least = jnp.min(values, keepdims=True)
        for row in range(rows):
            weights[row] = jnp.broadcast_to(values[row : row + 1, :], (blk, blk)).T
        acc[...] = jnp.zeros(acc.shape, jnp.float32)

        @pl.loop(0, work[groups + STEP])
        def _(step):
            for g in range(STEP):
                code = work[step * STEP + g]
                weight = weights[jnp.minimum(code // per_row, rows - 1)]
                for u in range(GROUP):
                    place = where_to[code * GROUP + u]
                    value = (tiles[code * GROUP + u] * weight).reshape(blk // 8, 8, blk)
                    acc[place] += jnp.sum(value, axis=0)

        for target in range(targets):
            sums[target : target + 1, :] = jnp.sum(acc[target], axis=0, keepdims=True)
        found = sums[...]
        reached = member[0:targets, :] > 0.5
        out[...] = jnp.where(
            reached, jnp.log2(jnp.where(reached, found, 1.0)) + (top - SHIFT), lowest
        )

        @pl.when(bad(found, least, reached))
        def _():
            slow_columns(ids, counts, x_hbm, y_hbm, log_weight, out)

    smem = pl.BlockSpec(memory_space=pltpu.SMEM)
    vmem = pl.BlockSpec(memory_space=pltpu.VMEM)
    hbm = pl.BlockSpec(memory_space=pltpu.HBM)
    f32, i32, bf16 = jnp.float32, jnp.int32, jnp.bfloat16
    limit = pltpu.CompilerParams(vmem_limit_bytes=24 * 1024 * 1024)

    def call(kernel, name, in_specs, outs, scratch):
        out_specs = [smem if o.memory_space == pltpu.SMEM else vmem for o in outs]
        run = pl.pallas_call(
            kernel, name=name, in_specs=in_specs, out_specs=out_specs, out_shape=outs,
            scratch_shapes=scratch, compiler_params=limit,
        )
        spaces = {id(smem): pltpu.SMEM, id(vmem): pltpu.VMEM, id(hbm): pltpu.HBM}

        def pinned(*operands):
            return run(
                *[
                    pltpu.with_memory_space_constraint(a, spaces[id(s)])
                    for a, s in zip(operands, in_specs, strict=True)
                ]
            )

        return pinned

    first_rows_call = call(
        first_rows,
        "first_rows",
        [hbm] * 7,
        [
            pltpu.VMEM((rows, blk), f32),
            pltpu.VMEM(((groups + 1) * GROUP, blk, blk), f32),
            pltpu.VMEM((targets, blk), f32),
            pltpu.VMEM((rows, blk), f32),
            pltpu.VMEM((padded, blk), f32),
            pltpu.VMEM((rows, blk), f32),
            pltpu.VMEM((targets, blk), f32),
            pltpu.SMEM((rows, slots), i32),
            pltpu.SMEM((rows,), i32),
            pltpu.SMEM((groups + STEP + 1,), i32),
            pltpu.SMEM(((groups + 1) * GROUP,), i32),
        ],
        [
            pltpu.VMEM((rows, feat, blk), bf16),
            pltpu.VMEM((targets, feat, blk), bf16),
            pltpu.VMEM((targets, blk), f32),
            pltpu.VMEM((rows, blk, blk), f32),
            pltpu.VMEM((padded, blk), f32),
            pltpu.VMEM((targets, blk), f32),
            pltpu.VMEM((rows, blk, feat), bf16),
            pltpu.VMEM((rows, blk), f32),
            pltpu.SemaphoreType.DMA((7,)),
        ],
    )
    later_rows_call = call(
        later_rows,
        "later_rows",
        [smem] * 4 + [vmem, hbm, hbm] + [vmem] * 3,
        [pltpu.VMEM((rows, blk), f32)],
        [
            pltpu.VMEM((rows + 1, blk, blk), f32),
            pltpu.VMEM((padded, blk), f32),
            pltpu.VMEM((targets, blk), f32),
            pltpu.VMEM((rows, blk), f32),
        ],
    )

    def columns_call(last):
        return call(
            functools.partial(columns, last),
            "last_columns" if last else "columns",
            [smem] * 4 + [vmem, hbm, hbm] + [vmem] * (5 if last else 4),
            [pltpu.VMEM((targets, blk), f32)] + ([pltpu.VMEM((rows, blk), f32)] if last else []),
            [
                pltpu.VMEM((padded, 8, blk), f32),
                pltpu.VMEM((rows, blk, blk), f32),
                pltpu.VMEM((targets, blk), f32),
                pltpu.VMEM((rows, blk), f32),
            ],
        )

    return first_rows_call, later_rows_call, columns_call


def joined_over_sources(part):
    size = lax.axis_size("src")
    step = 1
    while step < size:
        width = 4 if step == 1 and size % 4 == 0 else 2
        parts = [part] + [
            lax.ppermute(part, "src", [(i, i ^ (step * k)) for i in range(size)])
            for k in range(1, width)
        ]
        part = log_sum(parts)
        step *= width
    return part


def per_device(
    source_points,
    target_points,
    source_logmass,
    target_logmass,
    warm_potential,
    block_ids,
    live_counts,
):
    rows, feat, blk = source_points.shape
    targets = target_points.shape[0]
    slots = block_ids.shape[2]
    source_mass = source_logmass.reshape(rows, blk)
    target_mass = target_logmass.reshape(targets, blk)
    warm = warm_potential.reshape(targets, blk)
    first_rows, later_rows, columns = make_kernels(rows, targets, slots, feat, blk)
    swap = [(i, i ^ 1) for i in range(lax.axis_size("tgt"))]

    part, tiles, target_sq, source_sq, member, source_mass, target_mass, ids, counts, work, where_to = (
        first_rows(
            block_ids.reshape(rows, slots), live_counts.reshape(rows),
            source_points, target_points, warm, source_mass, target_mass,
        )
    )
    for sweep_index in range(ITERS):
        last = sweep_index == ITERS - 1
        common = (ids, counts, work, where_to, tiles, source_points, target_points)
        if sweep_index > 0:
            (part,) = later_rows(*common, merged, target_mass, target_sq)
        other = lax.ppermute(part, "tgt", swap)
        found = columns(last)(
            *common, part, other, source_mass, member, *([source_sq] if last else [])
        )
        merged = joined_over_sources(found[0])
    source_potential = found[1]
    log_total = jnp.where(
        merged > reach_limit, merged * UNSCALE - target_sq, 0.0
    )
    potential = epsilon * target_mass - log_total
    return (source_potential.reshape(-1), potential.reshape(-1))


def solution(mesh):
    in_specs = (
        P(("groups", "src"), None, None),
        P(("groups", "tgt"), None, None),
        P(("groups", "src")),
        P(("groups", "tgt")),
        P(("groups", "tgt")),
        P(("groups", "src"), "tgt", None),
        P(("groups", "src"), "tgt"),
    )
    out_specs = (P(("groups", "src")), P(("groups", "tgt")))
    return jax.shard_map(
        per_device, mesh=mesh, in_specs=in_specs, out_specs=out_specs, check_vma=False
    )
```

```python
import functools
import math

import jax
import jax.numpy as jnp
from jax import lax
from jax.experimental import pallas as pl
from jax.experimental.pallas import tpu as pltpu
from jax.sharding import PartitionSpec as P

ITERS = 2
epsilon = 0.1
lowest = -1.0e30
reach_limit = -1.0e29

LOG2E = math.log2(math.e)
SCALE = LOG2E / epsilon
UNSCALE = epsilon / LOG2E
SHIFT = 60.0
SUM_LOW = 2.0**-30
SUM_HIGH = 2.0**126
WEIGHT_LOW = 2.0**-125
GROUP = 4
STEP = 8
ROWS_STEP = 8


def log_add(first, second):
    highest = jnp.maximum(first, second)
    return highest + jnp.log2(jnp.exp2(first - highest) + jnp.exp2(second - highest))


def log_sum(parts):
    highest = functools.reduce(jnp.maximum, parts)
    total = functools.reduce(jnp.add, [jnp.exp2(part - highest) for part in parts])
    return highest + jnp.log2(total)


def make_kernels(rows, targets, slots, feat, blk):
    per_row = slots // GROUP
    groups = rows * per_row
    padded = targets + 8

    def tile_scores(x, y, row, target):
        return lax.dot_general(
            x[row], y[target], (((0,), (0,)), ((), ())), preferred_element_type=jnp.float32
        ) * (2.0 * SCALE)

    def slow_rows(ids, counts, x_hbm, y_hbm, weight_log, out):
        def run(x, y):
            pltpu.sync_copy(x_hbm, x)
            pltpu.sync_copy(y_hbm, y)

            @pl.loop(0, rows)
            def _(row):
                def body(k, state):
                    target = ids[row, k]
                    score = tile_scores(x, y, row, target) + weight_log[pl.ds(target, 1), :]
                    score = score.T
                    best = jnp.maximum(state[0], jnp.max(score, axis=0, keepdims=True))
                    total = state[1] * jnp.exp2(state[0] - best)
                    total += jnp.sum(jnp.exp2(score - best), axis=0, keepdims=True)
                    return best, total

                start = (jnp.full((1, blk), lowest, jnp.float32), jnp.zeros((1, blk), jnp.float32))
                best, total = lax.fori_loop(0, counts[row], body, start)
                out[pl.ds(row, 1), :] = best + jnp.log2(total)

        pl.run_scoped(
            run,
            pltpu.VMEM((rows, feat, blk), jnp.bfloat16),
            pltpu.VMEM((targets, feat, blk), jnp.bfloat16),
        )

    def slow_columns(ids, counts, x_hbm, y_hbm, weight_log, out):
        def run(x, y, total):
            pltpu.sync_copy(x_hbm, x)
            pltpu.sync_copy(y_hbm, y)
            out[...] = jnp.full((targets, blk), lowest, jnp.float32)
            total[...] = jnp.zeros((targets, blk), jnp.float32)

            @pl.loop(0, rows)
            def _(row):
                @pl.loop(0, counts[row])
                def _(k):
                    target = ids[row, k]
                    score = (tile_scores(x, y, row, target).T + weight_log[pl.ds(row, 1), :]).T
                    old = out[pl.ds(target, 1), :]
                    best = jnp.maximum(old, jnp.max(score, axis=0, keepdims=True))
                    add = jnp.sum(jnp.exp2(score - best), axis=0, keepdims=True)
                    total[pl.ds(target, 1), :] = (
                        total[pl.ds(target, 1), :] * jnp.exp2(old - best) + add
                    )
                    out[pl.ds(target, 1), :] = best

            best = out[...]
            reached = best > reach_limit
            out[...] = jnp.where(
                reached, best + jnp.log2(jnp.where(reached, total[...], 1.0)), lowest
            )

        pl.run_scoped(
            run,
            pltpu.VMEM((rows, feat, blk), jnp.bfloat16),
            pltpu.VMEM((targets, feat, blk), jnp.bfloat16),
            pltpu.VMEM((targets, blk), jnp.float32),
        )

    def list_groups(counts, work):
        def add(row, n):
            for g in range(per_row):
                work[n + g] = row * per_row + g
            return n + (counts[row] + GROUP - 1) // GROUP

        n = lax.fori_loop(0, rows, add, 0)
        for g in range(STEP):
            work[n + g] = groups
        work[groups + STEP] = (n + STEP - 1) // STEP

    def largest(values):
        return jnp.max(values, keepdims=True)

    def row_weights(log_weight, weights):
        top = largest(log_weight)
        values = jnp.exp2(log_weight - (top - SHIFT))
        weights[0:targets, :] = values
        weights[targets:padded, :] = jnp.zeros((padded - targets, blk), jnp.float32)
        return top, folded(jnp.where(values >= WEIGHT_LOW, 0.0, 1.0))

    def folded(values):
        return jnp.max(values.reshape(values.shape[0] // 8, 8, blk), axis=0)

    def bad(sums, low, mask=None):
        good = (sums >= SUM_LOW) & (sums <= SUM_HIGH)
        if mask is not None:
            good = good | jnp.logical_not(mask)
        return jnp.max(jnp.maximum(folded(jnp.where(good, 0.0, 1.0)), low)) > 0.5

    def turned(total):
        return jnp.sum(total.T.reshape(blk // 8, 8, blk), axis=0)

    def finish_rows(acc, top, least, log_weight, ids, counts, x_hbm, y_hbm, out, sums):
        for row in range(rows):
            sums[row : row + 1, :] = jnp.sum(acc[row], axis=0, keepdims=True)
        found = sums[...]
        out[...] = jnp.log2(found) + (top - SHIFT)

        @pl.when(bad(found, least))
        def _():
            slow_rows(ids, counts, x_hbm, y_hbm, log_weight, out)

    def first_rows(
        ids_hbm, counts_hbm, x_hbm, y_hbm, warm_hbm, source_mass_hbm, target_mass_hbm,
        out, tiles, target_sq, source_sq, member, source_mass, target_mass, ids, counts, work, where_to,
        x, y, warm, acc, weights, log_weight, x_rows, sums, sems,
    ):
        copies = [
            pltpu.make_async_copy(source, target, sems.at[i])
            for i, (source, target) in enumerate(
                (
                    (y_hbm, y),
                    (x_hbm, x),
                    (warm_hbm, warm),
                    (ids_hbm, ids),
                    (counts_hbm, counts),
                    (source_mass_hbm, source_mass),
                    (target_mass_hbm, target_mass),
                )
            )
        ]
        for copy in copies:
            copy.start()
        member[...] = jnp.zeros(member.shape, jnp.float32)
        for i in (4, 3, 2, 5, 6):
            copies[i].wait()
        list_groups(counts, work)
        for u in range(GROUP):
            where_to[groups * GROUP + u] = targets
        copies[1].wait()
        for row in range(rows):
            values = x[row].astype(jnp.float32)
            source_sq[row : row + 1, :] = jnp.sum(values * values, axis=0, keepdims=True)
            x_rows[row] = x[row].T
        copies[0].wait()
        for target in range(targets):
            values = y[target].astype(jnp.float32)
            target_sq[target : target + 1, :] = jnp.sum(values * values, axis=0, keepdims=True)
        log_weight[...] = (warm[...] - target_sq[...]) * SCALE
        top, least = row_weights(log_weight[...], weights)

        @pl.loop(0, rows // ROWS_STEP)
        def _(step):
            for part in range(ROWS_STEP):
                row = step * ROWS_STEP + part
                count = counts[row]
                total = jnp.zeros((blk, blk), jnp.float32)
                for k in range(slots):
                    target = ids[row, k]
                    place = jnp.where(k < count, target, targets)
                    where_to[row * slots + k] = place
                    product = jnp.dot(x_rows[row], y[target], preferred_element_type=jnp.float32)
                    value = jnp.exp2(product * (2.0 * SCALE))
                    tiles[row * slots + k] = value
                    total += value * weights[pl.ds(place, 1), :]
                    member[pl.ds(place, 1), :] = jnp.ones((1, blk), jnp.float32)
                acc[row] = turned(total)

        finish_rows(acc, top, least, log_weight, ids, counts, x_hbm, y_hbm, out, sums)

    def later_rows(
        ids, counts, work, where_to, tiles, x_hbm, y_hbm, merged_ref, target_mass, target_sq,
        out,
        acc, halves, weights, log_weight, sums,
    ):
        merged = merged_ref[...]
        reached = merged > reach_limit
        log_weight[...] = target_mass[...] * LOG2E - jnp.where(
            reached, merged, target_sq[...] * SCALE
        )
        top, least = row_weights(log_weight[...], weights)
        acc[...] = jnp.zeros(acc.shape, jnp.float32)

        @pl.loop(0, work[groups + STEP])
        def _(step):
            for g in range(STEP):
                code = work[step * STEP + g]
                row = code // per_row
                total = acc[row]
                for u in range(GROUP):
                    place = where_to[code * GROUP + u]
                    total += tiles[code * GROUP + u] * weights[pl.ds(place, 1), :]
                acc[row] = total

        for row in range(rows):
            halves[row] = turned(acc[row])
        finish_rows(halves, top, least, log_weight, ids, counts, x_hbm, y_hbm, out, sums)

    def columns(
        last, ids, counts, work, where_to, tiles, x_hbm, y_hbm, own, other, source_mass, member,
        *rest,
    ):
        if last:
            source_sq, out, potential, acc, weights, sums, log_weight = rest
        else:
            out, acc, weights, sums, log_weight = rest
        log_weight[...] = source_mass[...] * LOG2E - log_add(own[...], other[...])
        if last:
            potential[...] = log_weight[...] * UNSCALE + source_sq[...]
        top = largest(log_weight[...])
        values = jnp.exp2(log_weight[...] - (top - SHIFT))
        least = folded(jnp.where(values >= WEIGHT_LOW, 0.0, 1.0))
        for row in range(rows):
            weights[row] = jnp.broadcast_to(values[row : row + 1, :], (blk, blk)).T
        acc[...] = jnp.zeros(acc.shape, jnp.float32)

        @pl.loop(0, work[groups + STEP])
        def _(step):
            for g in range(STEP):
                code = work[step * STEP + g]
                weight = weights[jnp.minimum(code // per_row, rows - 1)]
                for u in range(GROUP):
                    place = where_to[code * GROUP + u]
                    value = (tiles[code * GROUP + u] * weight).reshape(blk // 8, 8, blk)
                    acc[place] += jnp.sum(value, axis=0)

        for target in range(targets):
            sums[target : target + 1, :] = jnp.sum(acc[target], axis=0, keepdims=True)
        found = sums[...]
        reached = member[0:targets, :] > 0.5
        out[...] = jnp.where(
            reached, jnp.log2(jnp.where(reached, found, 1.0)) + (top - SHIFT), lowest
        )

        @pl.when(bad(found, least, reached))
        def _():
            slow_columns(ids, counts, x_hbm, y_hbm, log_weight, out)

    smem = pl.BlockSpec(memory_space=pltpu.SMEM)
    vmem = pl.BlockSpec(memory_space=pltpu.VMEM)
    hbm = pl.BlockSpec(memory_space=pltpu.HBM)
    f32, i32, bf16 = jnp.float32, jnp.int32, jnp.bfloat16
    limit = pltpu.CompilerParams(vmem_limit_bytes=24 * 1024 * 1024)

    def call(kernel, name, in_specs, outs, scratch):
        out_specs = [smem if o.memory_space == pltpu.SMEM else vmem for o in outs]
        run = pl.pallas_call(
            kernel, name=name, in_specs=in_specs, out_specs=out_specs, out_shape=outs,
            scratch_shapes=scratch, compiler_params=limit,
        )
        spaces = {id(smem): pltpu.SMEM, id(vmem): pltpu.VMEM, id(hbm): pltpu.HBM}

        def pinned(*operands):
            return run(
                *[
                    pltpu.with_memory_space_constraint(a, spaces[id(s)])
                    for a, s in zip(operands, in_specs, strict=True)
                ]
            )

        return pinned

    first_rows_call = call(
        first_rows,
        "first_rows",
        [hbm] * 7,
        [
            pltpu.VMEM((rows, blk), f32),
            pltpu.VMEM(((groups + 1) * GROUP, blk, blk), f32),
            pltpu.VMEM((targets, blk), f32),
            pltpu.VMEM((rows, blk), f32),
            pltpu.VMEM((padded, blk), f32),
            pltpu.VMEM((rows, blk), f32),
            pltpu.VMEM((targets, blk), f32),
            pltpu.SMEM((rows, slots), i32),
            pltpu.SMEM((rows,), i32),
            pltpu.SMEM((groups + STEP + 1,), i32),
            pltpu.SMEM(((groups + 1) * GROUP,), i32),
        ],
        [
            pltpu.VMEM((rows, feat, blk), bf16),
            pltpu.VMEM((targets, feat, blk), bf16),
            pltpu.VMEM((targets, blk), f32),
            pltpu.VMEM((rows, 8, blk), f32),
            pltpu.VMEM((padded, blk), f32),
            pltpu.VMEM((targets, blk), f32),
            pltpu.VMEM((rows, blk, feat), bf16),
            pltpu.VMEM((rows, blk), f32),
            pltpu.SemaphoreType.DMA((7,)),
        ],
    )
    later_rows_call = call(
        later_rows,
        "later_rows",
        [smem] * 4 + [vmem, hbm, hbm] + [vmem] * 3,
        [pltpu.VMEM((rows, blk), f32)],
        [
            pltpu.VMEM((rows + 1, blk, blk), f32),
            pltpu.VMEM((rows, 8, blk), f32),
            pltpu.VMEM((padded, blk), f32),
            pltpu.VMEM((targets, blk), f32),
            pltpu.VMEM((rows, blk), f32),
        ],
    )

    def columns_call(last):
        return call(
            functools.partial(columns, last),
            "last_columns" if last else "columns",
            [smem] * 4 + [vmem, hbm, hbm] + [vmem] * (5 if last else 4),
            [pltpu.VMEM((targets, blk), f32)] + ([pltpu.VMEM((rows, blk), f32)] if last else []),
            [
                pltpu.VMEM((padded, 8, blk), f32),
                pltpu.VMEM((rows, blk, blk), f32),
                pltpu.VMEM((targets, blk), f32),
                pltpu.VMEM((rows, blk), f32),
            ],
        )

    return first_rows_call, later_rows_call, columns_call


def joined_over_sources(part):
    size = lax.axis_size("src")
    step = 1
    while step < size:
        width = 4 if step == 1 and size % 4 == 0 else 2
        parts = [part] + [
            lax.ppermute(part, "src", [(i, i ^ (step * k)) for i in range(size)])
            for k in range(1, width)
        ]
        part = log_sum(parts)
        step *= width
    return part


def per_device(
    source_points,
    target_points,
    source_logmass,
    target_logmass,
    warm_potential,
    block_ids,
    live_counts,
):
    rows, feat, blk = source_points.shape
    targets = target_points.shape[0]
    slots = block_ids.shape[2]
    source_mass = source_logmass.reshape(rows, blk)
    target_mass = target_logmass.reshape(targets, blk)
    warm = warm_potential.reshape(targets, blk)
    first_rows, later_rows, columns = make_kernels(rows, targets, slots, feat, blk)
    swap = [(i, i ^ 1) for i in range(lax.axis_size("tgt"))]

    part, tiles, target_sq, source_sq, member, source_mass, target_mass, ids, counts, work, where_to = (
        first_rows(
            block_ids.reshape(rows, slots), live_counts.reshape(rows),
            source_points, target_points, warm, source_mass, target_mass,
        )
    )
    for sweep_index in range(ITERS):
        last = sweep_index == ITERS - 1
        common = (ids, counts, work, where_to, tiles, source_points, target_points)
        if sweep_index > 0:
            (part,) = later_rows(*common, merged, target_mass, target_sq)
        other = lax.ppermute(part, "tgt", swap)
        found = columns(last)(
            *common, part, other, source_mass, member, *([source_sq] if last else [])
        )
        merged = joined_over_sources(found[0])
    source_potential = found[1]
    log_total = jnp.where(
        merged > reach_limit, merged * UNSCALE - target_sq, 0.0
    )
    potential = epsilon * target_mass - log_total
    return (source_potential.reshape(-1), potential.reshape(-1))


def solution(mesh):
    in_specs = (
        P(("groups", "src"), None, None),
        P(("groups", "tgt"), None, None),
        P(("groups", "src")),
        P(("groups", "tgt")),
        P(("groups", "tgt")),
        P(("groups", "src"), "tgt", None),
        P(("groups", "src"), "tgt"),
    )
    out_specs = (P(("groups", "src")), P(("groups", "tgt")))
    return jax.shard_map(
        per_device, mesh=mesh, in_specs=in_specs, out_specs=out_specs, check_vma=False
    )
```

```python
import functools
import math

import jax
import jax.numpy as jnp
from jax import lax
from jax.experimental import pallas as pl
from jax.experimental.pallas import tpu as pltpu
from jax.sharding import PartitionSpec as P

ITERS = 2
epsilon = 0.1
lowest = -1.0e30
reach_limit = -1.0e29

LOG2E = math.log2(math.e)
SCALE = LOG2E / epsilon
UNSCALE = epsilon / LOG2E
SHIFT = 60.0
SUM_LOW = 2.0**-30
SUM_HIGH = 2.0**126
WEIGHT_LOW = 2.0**-125
GROUP = 4
STEP = 8
ROWS_STEP = 8


def log_add(first, second):
    highest = jnp.maximum(first, second)
    return highest + jnp.log2(jnp.exp2(first - highest) + jnp.exp2(second - highest))


def log_sum(parts):
    highest = functools.reduce(jnp.maximum, parts)
    total = functools.reduce(jnp.add, [jnp.exp2(part - highest) for part in parts])
    return highest + jnp.log2(total)


def make_kernels(rows, targets, slots, feat, blk):
    per_row = slots // GROUP
    groups = rows * per_row
    padded = targets + 8

    def tile_scores(x, y, row, target):
        return lax.dot_general(
            x[row], y[target], (((0,), (0,)), ((), ())), preferred_element_type=jnp.float32
        ) * (2.0 * SCALE)

    def slow_rows(ids, counts, x_hbm, y_hbm, weight_log, out):
        def run(x, y):
            pltpu.sync_copy(x_hbm, x)
            pltpu.sync_copy(y_hbm, y)

            @pl.loop(0, rows)
            def _(row):
                def body(k, state):
                    target = ids[row, k]
                    score = tile_scores(x, y, row, target) + weight_log[pl.ds(target, 1), :]
                    score = score.T
                    best = jnp.maximum(state[0], jnp.max(score, axis=0, keepdims=True))
                    total = state[1] * jnp.exp2(state[0] - best)
                    total += jnp.sum(jnp.exp2(score - best), axis=0, keepdims=True)
                    return best, total

                start = (jnp.full((1, blk), lowest, jnp.float32), jnp.zeros((1, blk), jnp.float32))
                best, total = lax.fori_loop(0, counts[row], body, start)
                out[pl.ds(row, 1), :] = best + jnp.log2(total)

        pl.run_scoped(
            run,
            pltpu.VMEM((rows, feat, blk), jnp.bfloat16),
            pltpu.VMEM((targets, feat, blk), jnp.bfloat16),
        )

    def slow_columns(ids, counts, x_hbm, y_hbm, weight_log, out):
        def run(x, y, total):
            pltpu.sync_copy(x_hbm, x)
            pltpu.sync_copy(y_hbm, y)
            out[...] = jnp.full((targets, blk), lowest, jnp.float32)
            total[...] = jnp.zeros((targets, blk), jnp.float32)

            @pl.loop(0, rows)
            def _(row):
                @pl.loop(0, counts[row])
                def _(k):
                    target = ids[row, k]
                    score = (tile_scores(x, y, row, target).T + weight_log[pl.ds(row, 1), :]).T
                    old = out[pl.ds(target, 1), :]
                    best = jnp.maximum(old, jnp.max(score, axis=0, keepdims=True))
                    add = jnp.sum(jnp.exp2(score - best), axis=0, keepdims=True)
                    total[pl.ds(target, 1), :] = (
                        total[pl.ds(target, 1), :] * jnp.exp2(old - best) + add
                    )
                    out[pl.ds(target, 1), :] = best

            best = out[...]
            reached = best > reach_limit
            out[...] = jnp.where(
                reached, best + jnp.log2(jnp.where(reached, total[...], 1.0)), lowest
            )

        pl.run_scoped(
            run,
            pltpu.VMEM((rows, feat, blk), jnp.bfloat16),
            pltpu.VMEM((targets, feat, blk), jnp.bfloat16),
            pltpu.VMEM((targets, blk), jnp.float32),
        )

    def list_groups(counts, work):
        def add(row, n):
            for g in range(per_row):
                work[n + g] = row * per_row + g
            return n + (counts[row] + GROUP - 1) // GROUP

        n = lax.fori_loop(0, rows, add, 0)
        for g in range(STEP):
            work[n + g] = groups
        work[groups + STEP] = (n + STEP - 1) // STEP

    def largest(values):
        return jnp.max(values, keepdims=True)

    def row_weights(log_weight, weights):
        top = largest(log_weight)
        values = jnp.exp2(log_weight - (top - SHIFT))
        weights[0:targets, :] = values
        weights[targets:padded, :] = jnp.zeros((padded - targets, blk), jnp.float32)
        return top, folded(jnp.where(values >= WEIGHT_LOW, 0.0, 1.0))

    def folded(values):
        return jnp.max(values.reshape(values.shape[0] // 8, 8, blk), axis=0)

    def bad(sums, low, mask=None):
        good = (sums >= SUM_LOW) & (sums <= SUM_HIGH)
        if mask is not None:
            good = good | jnp.logical_not(mask)
        return jnp.max(jnp.maximum(folded(jnp.where(good, 0.0, 1.0)), low)) > 0.5

    def turned(total):
        return jnp.sum(total.T.reshape(blk // 8, 8, blk), axis=0)

    def finish_rows(acc, top, least, log_weight, ids, counts, x_hbm, y_hbm, out, sums):
        for row in range(rows):
            sums[row : row + 1, :] = jnp.sum(acc[row], axis=0, keepdims=True)
        found = sums[...]
        out[...] = jnp.log2(found) + (top - SHIFT)

        @pl.when(bad(found, least))
        def _():
            slow_rows(ids, counts, x_hbm, y_hbm, log_weight, out)

    def first_rows(
        ids_hbm, counts_hbm, x_hbm, y_hbm, warm_hbm, source_mass_hbm, target_mass_hbm,
        out, tiles, target_sq, source_sq, member, source_mass, target_mass, ids, counts, work, where_to,
        x, y, warm, acc, weights, log_weight, x_rows, sums, sems,
    ):
        copies = [
            pltpu.make_async_copy(source, target, sems.at[i])
            for i, (source, target) in enumerate(
                (
                    (y_hbm, y),
                    (x_hbm, x),
                    (warm_hbm, warm),
                    (ids_hbm, ids),
                    (counts_hbm, counts),
                    (source_mass_hbm, source_mass),
                    (target_mass_hbm, target_mass),
                )
            )
        ]
        for i in (4, 3, 1, 0, 2, 5, 6):
            copies[i].start()
        member[...] = jnp.zeros(member.shape, jnp.float32)
        for i in (4, 3):
            copies[i].wait()
        list_groups(counts, work)
        for u in range(GROUP):
            where_to[groups * GROUP + u] = targets
        copies[1].wait()
        for row in range(rows):
            values = x[row].astype(jnp.float32)
            source_sq[row : row + 1, :] = jnp.sum(values * values, axis=0, keepdims=True)
            x_rows[row] = x[row].T
        copies[2].wait()
        copies[0].wait()
        for target in range(targets):
            values = y[target].astype(jnp.float32)
            target_sq[target : target + 1, :] = jnp.sum(values * values, axis=0, keepdims=True)
        log_weight[...] = (warm[...] - target_sq[...]) * SCALE
        top, least = row_weights(log_weight[...], weights)

        @pl.loop(0, rows // ROWS_STEP)
        def _(step):
            for part in range(ROWS_STEP):
                row = step * ROWS_STEP + part
                count = counts[row]
                total = jnp.zeros((blk, blk), jnp.float32)
                places, wanted = [], []
                for k in range(slots):
                    target = ids[row, k]
                    place = jnp.where(k < count, target, targets)
                    where_to[row * slots + k] = place
                    places.append(place)
                    wanted.append(target)
                for k in range(0, slots, 2):
                    pair = jnp.concatenate([y[wanted[k]], y[wanted[k + 1]]], axis=1)
                    product = jnp.dot(x_rows[row], pair, preferred_element_type=jnp.float32)
                    value = jnp.exp2(product * (2.0 * SCALE))
                    tiles[row * slots + k] = value[:, :blk]
                    tiles[row * slots + k + 1] = value[:, blk:]
                    total += value[:, :blk] * weights[pl.ds(places[k], 1), :]
                    total += value[:, blk:] * weights[pl.ds(places[k + 1], 1), :]
                for k in range(slots):
                    member[pl.ds(places[k], 1), :] = jnp.ones((1, blk), jnp.float32)
                acc[row] = turned(total)

        copies[5].wait()
        copies[6].wait()
        finish_rows(acc, top, least, log_weight, ids, counts, x_hbm, y_hbm, out, sums)

    def later_rows(
        ids, counts, work, where_to, tiles, x_hbm, y_hbm, merged_ref, target_mass, target_sq,
        out,
        acc, halves, weights, log_weight, sums,
    ):
        merged = merged_ref[...]
        reached = merged > reach_limit
        log_weight[...] = target_mass[...] * LOG2E - jnp.where(
            reached, merged, target_sq[...] * SCALE
        )
        top, least = row_weights(log_weight[...], weights)
        acc[...] = jnp.zeros(acc.shape, jnp.float32)

        @pl.loop(0, work[groups + STEP])
        def _(step):
            for g in range(STEP):
                code = work[step * STEP + g]
                row = code // per_row
                total = acc[row]
                for u in range(GROUP):
                    place = where_to[code * GROUP + u]
                    total += tiles[code * GROUP + u] * weights[pl.ds(place, 1), :]
                acc[row] = total

        for row in range(rows):
            halves[row] = turned(acc[row])
        finish_rows(halves, top, least, log_weight, ids, counts, x_hbm, y_hbm, out, sums)

    def columns(
        last, ids, counts, work, where_to, tiles, x_hbm, y_hbm, own, other, source_mass, member,
        *rest,
    ):
        if last:
            source_sq, out, potential, acc, weights, sums, log_weight = rest
        else:
            out, acc, weights, sums, log_weight = rest
        log_weight[...] = source_mass[...] * LOG2E - log_add(own[...], other[...])
        if last:
            potential[...] = log_weight[...] * UNSCALE + source_sq[...]
        top = largest(log_weight[...])
        values = jnp.exp2(log_weight[...] - (top - SHIFT))
        least = folded(jnp.where(values >= WEIGHT_LOW, 0.0, 1.0))
        for row in range(rows):
            weights[row] = jnp.broadcast_to(values[row : row + 1, :], (blk, blk)).T
        acc[...] = jnp.zeros(acc.shape, jnp.float32)

        @pl.loop(0, work[groups + STEP])
        def _(step):
            for g in range(STEP):
                code = work[step * STEP + g]
                weight = weights[jnp.minimum(code // per_row, rows - 1)]
                for u in range(GROUP):
                    place = where_to[code * GROUP + u]
                    value = (tiles[code * GROUP + u] * weight).reshape(blk // 8, 8, blk)
                    acc[place] += jnp.sum(value, axis=0)

        for target in range(targets):
            sums[target : target + 1, :] = jnp.sum(acc[target], axis=0, keepdims=True)
        found = sums[...]
        reached = member[0:targets, :] > 0.5
        out[...] = jnp.where(
            reached, jnp.log2(jnp.where(reached, found, 1.0)) + (top - SHIFT), lowest
        )

        @pl.when(bad(found, least, reached))
        def _():
            slow_columns(ids, counts, x_hbm, y_hbm, log_weight, out)

    smem = pl.BlockSpec(memory_space=pltpu.SMEM)
    vmem = pl.BlockSpec(memory_space=pltpu.VMEM)
    hbm = pl.BlockSpec(memory_space=pltpu.HBM)
    f32, i32, bf16 = jnp.float32, jnp.int32, jnp.bfloat16
    limit = pltpu.CompilerParams(vmem_limit_bytes=24 * 1024 * 1024)

    def call(kernel, name, in_specs, outs, scratch):
        out_specs = [smem if o.memory_space == pltpu.SMEM else vmem for o in outs]
        run = pl.pallas_call(
            kernel, name=name, in_specs=in_specs, out_specs=out_specs, out_shape=outs,
            scratch_shapes=scratch, compiler_params=limit,
        )
        spaces = {id(smem): pltpu.SMEM, id(vmem): pltpu.VMEM, id(hbm): pltpu.HBM}

        def pinned(*operands):
            return run(
                *[
                    pltpu.with_memory_space_constraint(a, spaces[id(s)])
                    for a, s in zip(operands, in_specs, strict=True)
                ]
            )

        return pinned

    first_rows_call = call(
        first_rows,
        "first_rows",
        [hbm] * 7,
        [
            pltpu.VMEM((rows, blk), f32),
            pltpu.VMEM(((groups + 1) * GROUP, blk, blk), f32),
            pltpu.VMEM((targets, blk), f32),
            pltpu.VMEM((rows, blk), f32),
            pltpu.VMEM((padded, blk), f32),
            pltpu.VMEM((rows, blk), f32),
            pltpu.VMEM((targets, blk), f32),
            pltpu.SMEM((rows, slots), i32),
            pltpu.SMEM((rows,), i32),
            pltpu.SMEM((groups + STEP + 1,), i32),
            pltpu.SMEM(((groups + 1) * GROUP,), i32),
        ],
        [
            pltpu.VMEM((rows, feat, blk), bf16),
            pltpu.VMEM((targets, feat, blk), bf16),
            pltpu.VMEM((targets, blk), f32),
            pltpu.VMEM((rows, 8, blk), f32),
            pltpu.VMEM((padded, blk), f32),
            pltpu.VMEM((targets, blk), f32),
            pltpu.VMEM((rows, blk, feat), bf16),
            pltpu.VMEM((rows, blk), f32),
            pltpu.SemaphoreType.DMA((7,)),
        ],
    )
    later_rows_call = call(
        later_rows,
        "later_rows",
        [smem] * 4 + [vmem, hbm, hbm] + [vmem] * 3,
        [pltpu.VMEM((rows, blk), f32)],
        [
            pltpu.VMEM((rows + 1, blk, blk), f32),
            pltpu.VMEM((rows, 8, blk), f32),
            pltpu.VMEM((padded, blk), f32),
            pltpu.VMEM((targets, blk), f32),
            pltpu.VMEM((rows, blk), f32),
        ],
    )

    def columns_call(last):
        return call(
            functools.partial(columns, last),
            "last_columns" if last else "columns",
            [smem] * 4 + [vmem, hbm, hbm] + [vmem] * (5 if last else 4),
            [pltpu.VMEM((targets, blk), f32)] + ([pltpu.VMEM((rows, blk), f32)] if last else []),
            [
                pltpu.VMEM((padded, 8, blk), f32),
                pltpu.VMEM((rows, blk, blk), f32),
                pltpu.VMEM((targets, blk), f32),
                pltpu.VMEM((rows, blk), f32),
            ],
        )

    return first_rows_call, later_rows_call, columns_call


def joined_over_sources(part):
    size = lax.axis_size("src")
    step = 1
    while step < size:
        width = 4 if step == 1 and size % 4 == 0 else 2
        parts = [part] + [
            lax.ppermute(part, "src", [(i, i ^ (step * k)) for i in range(size)])
            for k in range(1, width)
        ]
        part = log_sum(parts)
        step *= width
    return part


def per_device(
    source_points,
    target_points,
    source_logmass,
    target_logmass,
    warm_potential,
    block_ids,
    live_counts,
):
    rows, feat, blk = source_points.shape
    targets = target_points.shape[0]
    slots = block_ids.shape[2]
    source_mass = source_logmass.reshape(rows, blk)
    target_mass = target_logmass.reshape(targets, blk)
    warm = warm_potential.reshape(targets, blk)
    first_rows, later_rows, columns = make_kernels(rows, targets, slots, feat, blk)
    swap = [(i, i ^ 1) for i in range(lax.axis_size("tgt"))]

    part, tiles, target_sq, source_sq, member, source_mass, target_mass, ids, counts, work, where_to = (
        first_rows(
            block_ids.reshape(rows, slots), live_counts.reshape(rows),
            source_points, target_points, warm, source_mass, target_mass,
        )
    )
    for sweep_index in range(ITERS):
        last = sweep_index == ITERS - 1
        common = (ids, counts, work, where_to, tiles, source_points, target_points)
        if sweep_index > 0:
            (part,) = later_rows(*common, merged, target_mass, target_sq)
        other = lax.ppermute(part, "tgt", swap)
        found = columns(last)(
            *common, part, other, source_mass, member, *([source_sq] if last else [])
        )
        merged = joined_over_sources(found[0])
    source_potential = found[1]
    log_total = jnp.where(
        merged > reach_limit, merged * UNSCALE - target_sq, 0.0
    )
    potential = epsilon * target_mass - log_total
    return (source_potential.reshape(-1), potential.reshape(-1))


def solution(mesh):
    in_specs = (
        P(("groups", "src"), None, None),
        P(("groups", "tgt"), None, None),
        P(("groups", "src")),
        P(("groups", "tgt")),
        P(("groups", "tgt")),
        P(("groups", "src"), "tgt", None),
        P(("groups", "src"), "tgt"),
    )
    out_specs = (P(("groups", "src")), P(("groups", "tgt")))
    return jax.shard_map(
        per_device, mesh=mesh, in_specs=in_specs, out_specs=out_specs, check_vma=False
    )
```

```python
import functools
import math

import jax
import jax.numpy as jnp
from jax import lax
from jax.experimental import pallas as pl
from jax.experimental.pallas import tpu as pltpu
from jax.sharding import PartitionSpec as P

ITERS = 2
epsilon = 0.1
lowest = -1.0e30
reach_limit = -1.0e29

LOG2E = math.log2(math.e)
SCALE = LOG2E / epsilon
UNSCALE = epsilon / LOG2E
SHIFT = 60.0
SUM_LOW = 2.0**-30
SUM_HIGH = 2.0**126
WEIGHT_LOW = 2.0**-125
GROUP = 4
STEP = 8
ROWS_STEP = 8


def log_add(first, second):
    highest = jnp.maximum(first, second)
    return highest + jnp.log2(jnp.exp2(first - highest) + jnp.exp2(second - highest))


def log_sum(parts):
    highest = functools.reduce(jnp.maximum, parts)
    total = functools.reduce(jnp.add, [jnp.exp2(part - highest) for part in parts])
    return highest + jnp.log2(total)


def make_kernels(rows, targets, slots, feat, blk):
    per_row = slots // GROUP
    groups = rows * per_row
    padded = targets + 8

    def tile_scores(x, y, row, target):
        return lax.dot_general(
            x[row], y[target], (((0,), (0,)), ((), ())), preferred_element_type=jnp.float32
        ) * (2.0 * SCALE)

    def slow_rows(ids, counts, x_hbm, y_hbm, weight_log, out):
        def run(x, y):
            pltpu.sync_copy(x_hbm, x)
            pltpu.sync_copy(y_hbm, y)

            @pl.loop(0, rows)
            def _(row):
                def body(k, state):
                    target = ids[row, k]
                    score = tile_scores(x, y, row, target) + weight_log[pl.ds(target, 1), :]
                    score = score.T
                    best = jnp.maximum(state[0], jnp.max(score, axis=0, keepdims=True))
                    total = state[1] * jnp.exp2(state[0] - best)
                    total += jnp.sum(jnp.exp2(score - best), axis=0, keepdims=True)
                    return best, total

                start = (jnp.full((1, blk), lowest, jnp.float32), jnp.zeros((1, blk), jnp.float32))
                best, total = lax.fori_loop(0, counts[row], body, start)
                out[pl.ds(row, 1), :] = best + jnp.log2(total)

        pl.run_scoped(
            run,
            pltpu.VMEM((rows, feat, blk), jnp.bfloat16),
            pltpu.VMEM((targets, feat, blk), jnp.bfloat16),
        )

    def slow_columns(ids, counts, x_hbm, y_hbm, weight_log, out):
        def run(x, y, total):
            pltpu.sync_copy(x_hbm, x)
            pltpu.sync_copy(y_hbm, y)
            out[...] = jnp.full((targets, blk), lowest, jnp.float32)
            total[...] = jnp.zeros((targets, blk), jnp.float32)

            @pl.loop(0, rows)
            def _(row):
                @pl.loop(0, counts[row])
                def _(k):
                    target = ids[row, k]
                    score = (tile_scores(x, y, row, target).T + weight_log[pl.ds(row, 1), :]).T
                    old = out[pl.ds(target, 1), :]
                    best = jnp.maximum(old, jnp.max(score, axis=0, keepdims=True))
                    add = jnp.sum(jnp.exp2(score - best), axis=0, keepdims=True)
                    total[pl.ds(target, 1), :] = (
                        total[pl.ds(target, 1), :] * jnp.exp2(old - best) + add
                    )
                    out[pl.ds(target, 1), :] = best

            best = out[...]
            reached = best > reach_limit
            out[...] = jnp.where(
                reached, best + jnp.log2(jnp.where(reached, total[...], 1.0)), lowest
            )

        pl.run_scoped(
            run,
            pltpu.VMEM((rows, feat, blk), jnp.bfloat16),
            pltpu.VMEM((targets, feat, blk), jnp.bfloat16),
            pltpu.VMEM((targets, blk), jnp.float32),
        )

    def list_groups(counts, work):
        def add(row, n):
            for g in range(per_row):
                work[n + g] = row * per_row + g
            return n + (counts[row] + GROUP - 1) // GROUP

        n = lax.fori_loop(0, rows, add, 0)
        for g in range(STEP):
            work[n + g] = groups
        work[groups + STEP] = (n + STEP - 1) // STEP

    def largest(values):
        return jnp.max(values, keepdims=True)

    def row_weights(log_weight, weights):
        top = largest(log_weight)
        values = jnp.exp2(log_weight - (top - SHIFT))
        weights[0:targets, :] = values
        weights[targets:padded, :] = jnp.zeros((padded - targets, blk), jnp.float32)
        return top, folded(jnp.where(values >= WEIGHT_LOW, 0.0, 1.0))

    def folded(values):
        return jnp.max(values.reshape(values.shape[0] // 8, 8, blk), axis=0)

    def bad(sums, low, mask=None):
        good = (sums >= SUM_LOW) & (sums <= SUM_HIGH)
        if mask is not None:
            good = good | jnp.logical_not(mask)
        return jnp.max(jnp.maximum(folded(jnp.where(good, 0.0, 1.0)), low)) > 0.5

    def turned(total):
        return jnp.sum(total.T.reshape(blk // 8, 8, blk), axis=0)

    def finish_rows(acc, top, least, log_weight, ids, counts, x_hbm, y_hbm, out, sums):
        for row in range(rows):
            sums[row : row + 1, :] = jnp.sum(acc[row], axis=0, keepdims=True)
        found = sums[...]
        out[...] = jnp.log2(found) + (top - SHIFT)

        @pl.when(bad(found, least))
        def _():
            slow_rows(ids, counts, x_hbm, y_hbm, log_weight, out)

    def first_rows(
        ids_hbm, counts_hbm, x_hbm, y_hbm, warm_hbm, source_mass_hbm, target_mass_hbm,
        out, tiles, target_sq, source_sq, member, source_mass, target_mass, ids, counts, work, where_to,
        x, y, warm, acc, weights, log_weight, x_rows, sums, sems,
    ):
        copies = [
            pltpu.make_async_copy(source, target, sems.at[i])
            for i, (source, target) in enumerate(
                (
                    (y_hbm, y),
                    (x_hbm, x),
                    (warm_hbm, warm),
                    (ids_hbm, ids),
                    (counts_hbm, counts),
                    (source_mass_hbm, source_mass),
                    (target_mass_hbm, target_mass),
                )
            )
        ]
        for i in (4, 3, 1, 0, 2, 5, 6):
            copies[i].start()
        member[...] = jnp.zeros(member.shape, jnp.float32)
        for i in (4, 3):
            copies[i].wait()
        list_groups(counts, work)
        for u in range(GROUP):
            where_to[groups * GROUP + u] = targets
        copies[1].wait()
        for row in range(rows):
            values = x[row].astype(jnp.float32)
            source_sq[row : row + 1, :] = jnp.sum(values * values, axis=0, keepdims=True)
            x_rows[row] = x[row].T
        copies[2].wait()
        copies[0].wait()
        for target in range(targets):
            values = y[target].astype(jnp.float32)
            target_sq[target : target + 1, :] = jnp.sum(values * values, axis=0, keepdims=True)
        log_weight[...] = (warm[...] - target_sq[...]) * SCALE
        top, least = row_weights(log_weight[...], weights)

        @pl.loop(0, rows // ROWS_STEP)
        def _(step):
            for part in range(ROWS_STEP):
                row = step * ROWS_STEP + part
                count = counts[row]
                total = jnp.zeros((blk, blk), jnp.float32)
                places, wanted = [], []
                for k in range(slots):
                    target = ids[row, k]
                    place = jnp.where(k < count, target, targets)
                    where_to[row * slots + k] = place
                    places.append(place)
                    wanted.append(target)
                for k in range(0, slots, 2):
                    pair = jnp.concatenate([y[wanted[k]], y[wanted[k + 1]]], axis=1)
                    product = jnp.dot(x_rows[row], pair, preferred_element_type=jnp.float32)
                    value = jnp.exp2(product * (2.0 * SCALE))
                    tiles[row * slots + k] = value[:, :blk]
                    tiles[row * slots + k + 1] = value[:, blk:]
                    total += value[:, :blk] * weights[pl.ds(places[k], 1), :]
                    total += value[:, blk:] * weights[pl.ds(places[k + 1], 1), :]
                for k in range(slots):
                    member[pl.ds(places[k], 1), :] = jnp.ones((1, blk), jnp.float32)
                acc[row] = turned(total)

        copies[5].wait()
        copies[6].wait()
        finish_rows(acc, top, least, log_weight, ids, counts, x_hbm, y_hbm, out, sums)

    def later_rows(
        ids, counts, work, where_to, tiles, x_hbm, y_hbm, merged_ref, other_ref, target_mass, target_sq,
        out,
        acc, halves, weights, log_weight, sums,
    ):
        merged = log_add(merged_ref[...], other_ref[...])
        reached = merged > reach_limit
        log_weight[...] = target_mass[...] * LOG2E - jnp.where(
            reached, merged, target_sq[...] * SCALE
        )
        top, least = row_weights(log_weight[...], weights)
        acc[...] = jnp.zeros(acc.shape, jnp.float32)

        @pl.loop(0, work[groups + STEP])
        def _(step):
            for g in range(STEP):
                code = work[step * STEP + g]
                row = code // per_row
                total = acc[row]
                for u in range(GROUP):
                    place = where_to[code * GROUP + u]
                    total += tiles[code * GROUP + u] * weights[pl.ds(place, 1), :]
                acc[row] = total

        for row in range(rows):
            halves[row] = turned(acc[row])
        finish_rows(halves, top, least, log_weight, ids, counts, x_hbm, y_hbm, out, sums)

    def columns(
        last, ids, counts, work, where_to, tiles, x_hbm, y_hbm, own, other, source_mass, member,
        *rest,
    ):
        if last:
            source_sq, out, potential, acc, weights, sums, log_weight = rest
        else:
            out, acc, weights, sums, log_weight = rest
        log_weight[...] = source_mass[...] * LOG2E - log_add(own[...], other[...])
        if last:
            potential[...] = log_weight[...] * UNSCALE + source_sq[...]
        top = largest(log_weight[...])
        values = jnp.exp2(log_weight[...] - (top - SHIFT))
        least = folded(jnp.where(values >= WEIGHT_LOW, 0.0, 1.0))
        for row in range(rows):
            weights[row] = jnp.broadcast_to(values[row : row + 1, :], (blk, blk)).T
        acc[...] = jnp.zeros(acc.shape, jnp.float32)

        @pl.loop(0, work[groups + STEP])
        def _(step):
            for g in range(STEP):
                code = work[step * STEP + g]
                weight = weights[jnp.minimum(code // per_row, rows - 1)]
                lines = [
                    jnp.sum((tiles[code * GROUP + u] * weight).reshape(blk // 8, 8, blk), axis=0)
                    for u in range(GROUP)
                ]
                for u in range(GROUP):
                    acc[where_to[code * GROUP + u]] += lines[u]

        for target in range(targets):
            sums[target : target + 1, :] = jnp.sum(acc[target], axis=0, keepdims=True)
        found = sums[...]
        reached = member[0:targets, :] > 0.5
        out[...] = jnp.where(
            reached, jnp.log2(jnp.where(reached, found, 1.0)) + (top - SHIFT), lowest
        )

        @pl.when(bad(found, least, reached))
        def _():
            slow_columns(ids, counts, x_hbm, y_hbm, log_weight, out)

    smem = pl.BlockSpec(memory_space=pltpu.SMEM)
    vmem = pl.BlockSpec(memory_space=pltpu.VMEM)
    hbm = pl.BlockSpec(memory_space=pltpu.HBM)
    f32, i32, bf16 = jnp.float32, jnp.int32, jnp.bfloat16
    limit = pltpu.CompilerParams(vmem_limit_bytes=24 * 1024 * 1024)

    def call(kernel, name, in_specs, outs, scratch):
        out_specs = [smem if o.memory_space == pltpu.SMEM else vmem for o in outs]
        run = pl.pallas_call(
            kernel, name=name, in_specs=in_specs, out_specs=out_specs, out_shape=outs,
            scratch_shapes=scratch, compiler_params=limit,
        )
        spaces = {id(smem): pltpu.SMEM, id(vmem): pltpu.VMEM, id(hbm): pltpu.HBM}

        def pinned(*operands):
            return run(
                *[
                    pltpu.with_memory_space_constraint(a, spaces[id(s)])
                    for a, s in zip(operands, in_specs, strict=True)
                ]
            )

        return pinned

    first_rows_call = call(
        first_rows,
        "first_rows",
        [hbm] * 7,
        [
            pltpu.VMEM((rows, blk), f32),
            pltpu.VMEM(((groups + 1) * GROUP, blk, blk), f32),
            pltpu.VMEM((targets, blk), f32),
            pltpu.VMEM((rows, blk), f32),
            pltpu.VMEM((padded, blk), f32),
            pltpu.VMEM((rows, blk), f32),
            pltpu.VMEM((targets, blk), f32),
            pltpu.SMEM((rows, slots), i32),
            pltpu.SMEM((rows,), i32),
            pltpu.SMEM((groups + STEP + 1,), i32),
            pltpu.SMEM(((groups + 1) * GROUP,), i32),
        ],
        [
            pltpu.VMEM((rows, feat, blk), bf16),
            pltpu.VMEM((targets, feat, blk), bf16),
            pltpu.VMEM((targets, blk), f32),
            pltpu.VMEM((rows, 8, blk), f32),
            pltpu.VMEM((padded, blk), f32),
            pltpu.VMEM((targets, blk), f32),
            pltpu.VMEM((rows, blk, feat), bf16),
            pltpu.VMEM((rows, blk), f32),
            pltpu.SemaphoreType.DMA((7,)),
        ],
    )
    later_rows_call = call(
        later_rows,
        "later_rows",
        [smem] * 4 + [vmem, hbm, hbm] + [vmem] * 4,
        [pltpu.VMEM((rows, blk), f32)],
        [
            pltpu.VMEM((rows + 1, blk, blk), f32),
            pltpu.VMEM((rows, 8, blk), f32),
            pltpu.VMEM((padded, blk), f32),
            pltpu.VMEM((targets, blk), f32),
            pltpu.VMEM((rows, blk), f32),
        ],
    )

    def columns_call(last):
        return call(
            functools.partial(columns, last),
            "last_columns" if last else "columns",
            [smem] * 4 + [vmem, hbm, hbm] + [vmem] * (5 if last else 4),
            [pltpu.VMEM((targets, blk), f32)] + ([pltpu.VMEM((rows, blk), f32)] if last else []),
            [
                pltpu.VMEM((padded, 8, blk), f32),
                pltpu.VMEM((rows, blk, blk), f32),
                pltpu.VMEM((targets, blk), f32),
                pltpu.VMEM((rows, blk), f32),
            ],
        )

    return first_rows_call, later_rows_call, columns_call


def joined_over_sources(part):
    size = lax.axis_size("src")
    step = 1
    while step < size:
        width = 4 if step == 1 and size % 4 == 0 else 2
        parts = [part] + [
            lax.ppermute(part, "src", [(i, i ^ (step * k)) for i in range(size)])
            for k in range(1, width)
        ]
        step *= width
        if step < size:
            part = log_sum(parts)
    return parts


def per_device(
    source_points,
    target_points,
    source_logmass,
    target_logmass,
    warm_potential,
    block_ids,
    live_counts,
):
    rows, feat, blk = source_points.shape
    targets = target_points.shape[0]
    slots = block_ids.shape[2]
    source_mass = source_logmass.reshape(rows, blk)
    target_mass = target_logmass.reshape(targets, blk)
    warm = warm_potential.reshape(targets, blk)
    first_rows, later_rows, columns = make_kernels(rows, targets, slots, feat, blk)
    swap = [(i, i ^ 1) for i in range(lax.axis_size("tgt"))]

    part, tiles, target_sq, source_sq, member, source_mass, target_mass, ids, counts, work, where_to = (
        first_rows(
            block_ids.reshape(rows, slots), live_counts.reshape(rows),
            source_points, target_points, warm, source_mass, target_mass,
        )
    )
    for sweep_index in range(ITERS):
        last = sweep_index == ITERS - 1
        common = (ids, counts, work, where_to, tiles, source_points, target_points)
        if sweep_index > 0:
            (part,) = later_rows(*common, *pair, target_mass, target_sq)
        other = lax.ppermute(part, "tgt", swap)
        found = columns(last)(
            *common, part, other, source_mass, member, *([source_sq] if last else [])
        )
        pair = joined_over_sources(found[0])
    merged = log_add(*pair)
    source_potential = found[1]
    log_total = jnp.where(
        merged > reach_limit, merged * UNSCALE - target_sq, 0.0
    )
    potential = epsilon * target_mass - log_total
    return (source_potential.reshape(-1), potential.reshape(-1))


def solution(mesh):
    in_specs = (
        P(("groups", "src"), None, None),
        P(("groups", "tgt"), None, None),
        P(("groups", "src")),
        P(("groups", "tgt")),
        P(("groups", "tgt")),
        P(("groups", "src"), "tgt", None),
        P(("groups", "src"), "tgt"),
    )
    out_specs = (P(("groups", "src")), P(("groups", "tgt")))
    return jax.shard_map(
        per_device, mesh=mesh, in_specs=in_specs, out_specs=out_specs, check_vma=False
    )
```
